32 devices in a mesh: cx: 8 (over z, x), cy: 4 (over y, core).
Axes of the slice: x: 2, y: 2, z: 4, core: 2. Of those that a mesh axis runs over, the one named last changes fastest.
Arguments:
- cell_pos: float32 [32, 16, 3, 1024], P('cx', 'cy'), may hold values from -6 to 6
- cell_drag: float32 [32, 16], P('cx', 'cy'), may hold values from 0.2 to 2
- cell_near: int32 [32, 16, 2], P('cx', 'cy'), may hold values from 0 to 511, as said below
- analysis: bfloat16 [1024, 1024], replicated, may hold values from -0.1875 to 0.1875
- stiffness: float32 [1024], replicated, may hold values from 0.1 to 1
- synthesis: bfloat16 [1024, 1024], replicated, may hold values from -0.1875 to 0.1875
- wall_pos: float32 [256, 3, 256], P(('cx', 'cy')), may hold values from -9 to 9
- wall_normal: float32 [256, 3, 256], P(('cx', 'cy')), may hold values from -6 to 6
- wall_weight: float32 [256, 256], P(('cx', 'cy')), may hold values from 0.02 to 0.2
- density: float32 [256, 3, 256], P(('cx', 'cy')), may hold values from -6 to 6
- patch_near: int32 [256, 4], P(('cx', 'cy')), may hold values from 0 to 255, as said below
- cell_to_patch: int32 [256, 2], P(('cx', 'cy')), may hold values from 0 to 511, as said below
Outputs:
- moved_cells: float32 [32, 16, 3, 1024], P('cx', 'cy')
- density_next: float32 [256, 3, 256], P(('cx', 'cy'))
The draws below stay inside these ranges and needn't reach their ends.
Inputs may be any that keep to these rules, and one draw needn't show every extreme that they name: `cell_near`: each entry is the row-major index (row times 16 plus column) of a cell whose grid row and column differ from the listing cell's by at most 3 each, cyclically, and never the listing cell itself. `cell_to_patch`: for the patches of block b (patches b * 8 to b * 8 + 7), with b = i * 4 + j, each entry is the row-major index of a cell whose row lies within 3 of the rows i * 4 to i * 4 + 3 and whose column lies within 3 of the columns j * 4 to j * 4 + 3, cyclically. `patch_near`: each entry is a patch of the listing patch's block of 8 or of the two blocks beside it, cyclically, and never the listing patch itself.
All inputs are finite; a program needn't handle non-finite values.
Results may differ from the reference program's by a relative error of at most 0.0041.
Values sent between devices are 32-bit elements; how exact they have to be, the bound alone decides.
A program may use at most 64 MiB of HBM per device.

```python
import math
import jax
import jax.numpy as jnp
from jax import lax

P_SIZE = 1024
Q = 1024
PP = 256
HALO = 3
NEAR = 2
CPNEAR = 2
PNEAR = 4
CXD = 4
CYD = 4
PATCH_DEV = 8
NXC = 32
NYC = 16
PATCHES = 256
N_CY = 4


def draw_cell_near(key, part):
    window = 2 * HALO + 1
    centre = HALO * window + HALO
    picked = jax.random.randint(key, (NXC, NYC, NEAR), 0, window * window - 1)
    picked = picked + (picked >= centre).astype(jnp.int32)
    shift_row = picked // window - HALO
    shift_col = picked % window - HALO
    grid_row = jnp.arange(NXC, dtype=jnp.int32)[:, None, None]
    grid_col = jnp.arange(NYC, dtype=jnp.int32)[None, :, None]
    return ((grid_row + shift_row) % NXC * NYC + (grid_col + shift_col) % NYC).astype(jnp.int32)


def draw_cell_to_patch(key, part):
    first_key, second_key = jax.random.split(jax.random.fold_in(key, 7))
    patch_ids = jnp.arange(PATCHES, dtype=jnp.int32)[:, None]
    block = patch_ids // PATCH_DEV
    block_row = block // N_CY
    block_col = block % N_CY
    offset_row = jax.random.randint(first_key, (PATCHES, CPNEAR), 0, CXD + 2 * HALO)
    offset_col = jax.random.randint(second_key, (PATCHES, CPNEAR), 0, CYD + 2 * HALO)
    grid_row = (block_row * CXD - HALO + offset_row) % NXC
    grid_col = (block_col * CYD - HALO + offset_col) % NYC
    return (grid_row * NYC + grid_col).astype(jnp.int32)


def draw_patch_near(key, part):
    picked = jax.random.randint(jax.random.fold_in(key, 11), (PATCHES, PNEAR), 0, 3 * PATCH_DEV - 1)
    patch_ids = jnp.arange(PATCHES, dtype=jnp.int32)[:, None]
    itself = patch_ids % PATCH_DEV + PATCH_DEV
    picked = picked + (picked >= itself).astype(jnp.int32)
    base = patch_ids // PATCH_DEV * PATCH_DEV - PATCH_DEV
    return ((base + picked) % PATCHES).astype(jnp.int32)


def steps_of(rng, dims, shards, least, top_value):
    gain, own = 1.0, jax.random.fold_in(rng, 6)
    for position, shards_of in shards:
        heights = jnp.exp(jax.random.uniform(jax.random.fold_in(own, position), (shards_of,), jnp.float32, least / len(shards), top_value / len(shards)))
        gain = gain * jnp.repeat(heights, dims[position] // shards_of).reshape([-1 if axis == position else 1 for axis in range(len(dims))])
    return gain


def gaussian(rng, extent, deviation, most, shards=(), held_as=jnp.bfloat16):
    result = deviation * jax.random.normal(rng, extent, jnp.float32)
    if shards:
        result = result * steps_of(rng, extent, shards, -0.22, 0.18)
    return jnp.clip(result, -most, most).astype(held_as)


def setup_inputs(seed: int = 0) -> dict:
    splits = jax.random.split(jax.random.key(seed), 13)
    cell_pos = gaussian(splits[0], (NXC, NYC, 3, P_SIZE), 1.0, 6.0, ((0, 8), (1, 4)), jnp.float32)
    cell_drag = jnp.clip(jnp.exp(math.log(2.0) - 2.3025851 * jax.random.uniform(splits[1], (NXC, NYC), jnp.float32) ** steps_of(splits[1], (NXC, NYC), ((0, 8), (1, 4)), -0.2, 0.2)), 0.2, 2.0)
    cell_near = draw_cell_near(jax.random.fold_in(splits[12], 71), 0)
    analysis = gaussian(splits[3], (P_SIZE, Q), P_SIZE ** -0.5, 0.1875)
    stiffness = jnp.clip(jnp.exp(jax.random.uniform(splits[4], (Q,), jnp.float32, math.log(0.1), math.log(1.0))), 0.1, 1.0)
    synthesis = gaussian(splits[5], (Q, P_SIZE), Q ** -0.5, 0.1875)
    wall_pos = gaussian(splits[6], (PATCHES, 3, PP), 1.5, 9.0, ((0, 32),), jnp.float32)
    wall_normal = gaussian(splits[7], (PATCHES, 3, PP), 1.0, 6.0, ((0, 32),), jnp.float32)
    wall_weight = jnp.clip(jnp.exp(math.log(0.2) - 2.3025851 * jax.random.uniform(splits[8], (PATCHES, PP), jnp.float32) ** steps_of(splits[8], (PATCHES, PP), ((0, 32),), -0.2, 0.2)), 0.02, 0.2)
    density = gaussian(splits[9], (PATCHES, 3, PP), 1.0, 6.0, ((0, 32),), jnp.float32)
    patch_near = draw_patch_near(jax.random.fold_in(splits[12], 71), 0)
    cell_to_patch = draw_cell_to_patch(jax.random.fold_in(splits[12], 71), 0)
    return dict(cell_pos=cell_pos, cell_drag=cell_drag, cell_near=cell_near, analysis=analysis, stiffness=stiffness, synthesis=synthesis, wall_pos=wall_pos, wall_normal=wall_normal, wall_weight=wall_weight, density=density, patch_near=patch_near, cell_to_patch=cell_to_patch)


soften = 0.25
stokes_scale = 1.0 / (8.0 * math.pi)
layer_scale = 3.0 / (4.0 * math.pi)

def membrane(positions, analysis, stiffness, synthesis):
    points = positions.shape[-1]
    centred = positions - lax.optimization_barrier(jnp.mean(positions, axis=-1, keepdims=True))
    flat = centred.reshape(-1, points).astype(jnp.bfloat16)
    coeff = jnp.dot(flat, analysis, preferred_element_type=jnp.float32)
    scaled = (coeff * stiffness[None, :]).astype(jnp.bfloat16)
    force = -jnp.dot(scaled, synthesis, preferred_element_type=jnp.float32)
    return force.reshape(positions.shape)

def stokeslet(targets, sources, forces):
    delta_x = targets[0][:, None] - sources[0][None, :]
    delta_y = targets[1][:, None] - sources[1][None, :]
    delta_z = targets[2][:, None] - sources[2][None, :]
    square = delta_x * delta_x + delta_y * delta_y + delta_z * delta_z + soften
    factor = lax.rsqrt(square) / square
    along = delta_x * forces[0][None, :] + delta_y * forces[1][None, :] + delta_z * forces[2][None, :]
    direct = (square + soften) * factor
    tangent = along * factor
    out_x = lax.optimization_barrier(jnp.sum(direct * forces[0][None, :] + tangent * delta_x, axis=1))
    out_y = lax.optimization_barrier(jnp.sum(direct * forces[1][None, :] + tangent * delta_y, axis=1))
    out_z = lax.optimization_barrier(jnp.sum(direct * forces[2][None, :] + tangent * delta_z, axis=1))
    return stokes_scale * jnp.stack([out_x, out_y, out_z])

def double_layer(targets, sources, normals, weights, values):
    delta_x = targets[0][:, None] - sources[0][None, :]
    delta_y = targets[1][:, None] - sources[1][None, :]
    delta_z = targets[2][:, None] - sources[2][None, :]
    square = delta_x * delta_x + delta_y * delta_y + delta_z * delta_z + soften
    factor = lax.rsqrt(square) / (square * square)
    along_q = delta_x * values[0][None, :] + delta_y * values[1][None, :] + delta_z * values[2][None, :]
    along_n = delta_x * normals[0][None, :] + delta_y * normals[1][None, :] + delta_z * normals[2][None, :]
    scalar = -layer_scale * weights[None, :] * along_q * along_n * factor
    return jnp.stack([lax.optimization_barrier(jnp.sum(scalar * delta_x, axis=1)), lax.optimization_barrier(jnp.sum(scalar * delta_y, axis=1)), lax.optimization_barrier(jnp.sum(scalar * delta_z, axis=1))])

def spread(picked):
    count = picked.shape[0]
    return jnp.swapaxes(picked, 0, 1).reshape(3, count * picked.shape[-1])

def reference(cell_pos, cell_drag, cell_near, analysis, stiffness, synthesis, wall_pos, wall_normal, wall_weight, density, patch_near, cell_to_patch):
    forces = membrane(cell_pos, analysis, stiffness, synthesis)
    flat_pos = cell_pos.reshape(NXC * NYC, 3, P_SIZE)
    flat_force = forces.reshape(NXC * NYC, 3, P_SIZE)

    def one_cell(target, neighbours):
        return stokeslet(target, spread(flat_pos[neighbours]), spread(flat_force[neighbours]))

    def one_row(pieces):
        return jax.vmap(one_cell)(pieces[0], pieces[1])
    near = lax.map(one_row, (cell_pos, cell_near))
    velocity = cell_drag[:, :, None, None] * forces + near
    speed = jnp.sqrt(lax.optimization_barrier(jnp.sum(velocity * velocity, axis=2)))
    step = 1.0 / (jnp.max(speed) + 1e-06)
    moved_cells = cell_pos + step * velocity

    def wall_from_cells(pieces):
        target, listed = pieces
        return stokeslet(target, spread(flat_pos[listed]), spread(flat_force[listed]))
    wall_velocity = lax.map(wall_from_cells, (wall_pos, cell_to_patch))
    patch_ids = jnp.arange(PATCHES, dtype=jnp.int32)

    def layer_patch(pieces):
        own, target, listed = pieces
        chosen = jnp.concatenate([own[None], listed]).astype(jnp.int32)
        return double_layer(target, spread(wall_pos[chosen]), spread(wall_normal[chosen]), wall_weight[chosen].reshape(-1), spread(density[chosen]))
    layer = lax.map(layer_patch, (patch_ids, wall_pos, patch_near))
    density_next = 2.0 * layer + 2.0 * wall_velocity
    return (moved_cells, density_next)
```

```python
import functools
import math

import jax
import jax.numpy as jnp
from jax import lax
from jax.experimental import pallas as pl
from jax.experimental.pallas import tpu as pltpu
from jax.sharding import PartitionSpec as P

HALO = 3
CHUNK = 256

soften = 0.25
stokes_scale = 1.0 / (8.0 * math.pi)
layer_scale = 3.0 / (4.0 * math.pi)

MESH = pl.DeviceIdType.MESH
f32 = jnp.float32
bf16 = jnp.bfloat16


def with_halo(value, sides, width):
    for axis, dim in sides:
        size, length = (lax.axis_size(axis), value.shape[dim])
        up = [(i, (i + 1) % size) for i in range(size)]
        down = [(j, i) for i, j in up]
        last = lax.slice_in_dim(value, length - width, length, axis=dim)
        initial = lax.slice_in_dim(value, 0, width, axis=dim)
        before = lax.ppermute(last, axis, up)
        after = lax.ppermute(initial, axis, down)
        value = jnp.concatenate([before, value, after], axis=dim)
    return value


def membrane(positions, analysis, stiffness, synthesis):
    points = positions.shape[-1]
    centred = positions - jnp.mean(positions, axis=-1, keepdims=True)
    flat = centred.reshape(-1, points).astype(jnp.bfloat16)
    coeff = jnp.dot(flat, analysis, preferred_element_type=jnp.float32)
    scaled = (coeff * stiffness[None, :]).astype(jnp.bfloat16)
    force = -jnp.dot(scaled, synthesis, preferred_element_type=jnp.float32)
    return force.reshape(positions.shape)


def local_slot(global_id, first_row, first_col, all_rows, all_cols, ext_cols):
    grid_row = global_id // all_cols
    grid_col = global_id % all_cols
    local_row = (grid_row - first_row + HALO) % all_rows
    local_col = (grid_col - first_col + HALO) % all_cols
    return local_row * ext_cols + local_col


def pieces(value):
    high = value.astype(bf16).astype(f32)
    rest = value - high
    middle = rest.astype(bf16).astype(f32)
    return high, middle, rest - middle


def rows8(points):
    return [jnp.broadcast_to(points[i : i + 1, :], (8, points.shape[1])) for i in range(3)]


def pick(row, values):
    out = jnp.zeros_like(values[0])
    for i, value in enumerate(values):
        out = jnp.where(row == i, value, out)
    return out


def target_features(points):
    x0, x1, x2 = rows8(points)
    row = lax.broadcasted_iota(jnp.int32, x0.shape, 0)
    square = x0 * x0 + x1 * x1 + x2 * x2
    high, middle, low = pieces(pick(row, [x0, x1, x2, square, jnp.ones_like(x0)]))
    return jnp.concatenate([high, high, middle, high, low, middle], axis=0).astype(bf16)


def source_side(value):
    high, middle, low = pieces(value)
    stacked = jnp.concatenate([high, middle, high, low, high, middle], axis=0)
    return stacked.T.astype(bf16)


def distance_features(y, row):
    y0, y1, y2 = y
    square = y0 * y0 + y1 * y1 + y2 * y2 + soften
    return source_side(pick(row, [-2.0 * y0, -2.0 * y1, -2.0 * y2, jnp.ones_like(y0), square]))


def stokes_prepare(source, force, side_ref, direct_ref, coef_ref, base):
    y = rows8(source)
    f = rows8(force)
    row = lax.broadcasted_iota(jnp.int32, y[0].shape, 0)
    side = distance_features(y, row)
    along = y[0] * f[0] + y[1] * f[1] + y[2] * f[2]
    f8 = pick(row % 4, [f[0], f[1], f[2], along])
    first = f8 * jnp.where(row < 4, 1.0, y[0])
    second = f8 * jnp.where(row < 4, y[1], y[2])
    direct = jnp.concatenate(pieces(f8)[:2], axis=0).astype(bf16)
    h1, m1, l1 = pieces(first)
    h2, m2, l2 = pieces(second)
    coef = jnp.concatenate([h1, h2, m1, m2, l1, l2], axis=0).astype(bf16)
    for c in range(side.shape[0] // CHUNK):
        part = slice(c * CHUNK, (c + 1) * CHUNK)
        side_ref[base + c] = side[part]
        direct_ref[base + c] = direct[:, part]
        coef_ref[base + c] = coef[:, part]


def stokes_chunks(features, side_ref, direct_ref, coef_ref, acc_ref, chunks, width):
    total = features.shape[1]
    acc_ref[...] = jnp.zeros_like(acc_ref)

    def step(c, carry):
        side = side_ref[c]
        direct = direct_ref[c]
        coef = coef_ref[c]
        for t in range(total // width):
            part = slice(t * width, (t + 1) * width)
            s = jnp.dot(side, features[:, part], preferred_element_type=f32)
            root = lax.rsqrt(s)
            cube = (root * root * root).astype(bf16)
            acc_ref[0:16, part] += jnp.dot(direct, root.astype(bf16), preferred_element_type=f32)
            acc_ref[16:64, part] += jnp.dot(coef, cube, preferred_element_type=f32)
        return carry

    lax.fori_loop(0, chunks, step, 0)


def stokes_finish(target, acc_ref):
    x = [target[i : i + 1, :] for i in range(3)]
    direct = acc_ref[0:8, :] + acc_ref[8:16, :]
    low = acc_ref[16:24, :] + (acc_ref[32:40, :] + acc_ref[48:56, :])
    high = acc_ref[24:32, :] + (acc_ref[40:48, :] + acc_ref[56:64, :])

    def contract(block, at):
        out = -block[at + 3 : at + 4]
        for j in range(3):
            out = out + x[j] * block[at + j : at + j + 1]
        return out

    line = contract(low, 0)
    turned = [contract(low, 4), contract(high, 0), contract(high, 4)]
    return [
        stokes_scale * (direct[i : i + 1] + soften * low[i : i + 1] + x[i] * line - turned[i])
        for i in range(3)
    ]


def cell_kernel(
    slot_ref, own_ref, drag_ref, target_ref, pos_ref, force_ref, out_ref, top_ref,
    side_ref, direct_ref, coef_ref, acc_ref, *, near
):
    cell = pl.program_id(0)
    target = target_ref[0]
    per_cell = pos_ref.shape[2] // CHUNK
    features = target_features(target)
    for n in range(near):
        slot = slot_ref[cell, n]
        stokes_prepare(pos_ref[slot], force_ref[slot], side_ref, direct_ref, coef_ref, n * per_cell)
    stokes_chunks(features, side_ref, direct_ref, coef_ref, acc_ref, near * per_cell, 256)
    own = force_ref[own_ref[cell]]
    drag = drag_ref[cell]
    parts = stokes_finish(target, acc_ref)
    square = jnp.zeros_like(parts[0])
    for i in range(3):
        value = drag * own[i : i + 1] + parts[i]
        out_ref[0, i : i + 1, :] = value
        square = square + value * value
    best = jnp.broadcast_to(jnp.max(square, axis=1, keepdims=True), (1, 128))

    @pl.when(cell == 0)
    def _():
        top_ref[...] = best

    @pl.when(cell > 0)
    def _():
        top_ref[...] = jnp.maximum(top_ref[...], best)


def cell_velocity(cells, drag, near_slots, own_slots, flat_pos, flat_force):
    count, _, points = cells.shape
    near = near_slots.shape[1]
    chunks = near * points // CHUNK
    whole = pl.BlockSpec(flat_pos.shape, lambda i, *_: (0, 0, 0), pipeline_mode=pl.Buffered(1))
    one = pl.BlockSpec((1, 3, points), lambda i, *_: (i, 0, 0))
    return pl.pallas_call(
        functools.partial(cell_kernel, near=near),
        grid_spec=pltpu.PrefetchScalarGridSpec(
            num_scalar_prefetch=3,
            grid=(count,),
            in_specs=[one, whole, whole],
            out_specs=[one, pl.BlockSpec((1, 128), lambda i, *_: (0, 0))],
            scratch_shapes=[
                pltpu.VMEM((chunks, CHUNK, 48), bf16),
                pltpu.VMEM((chunks, 16, CHUNK), bf16),
                pltpu.VMEM((chunks, 48, CHUNK), bf16),
                pltpu.VMEM((64, points), f32),
            ],
        ),
        out_shape=(
            jax.ShapeDtypeStruct(cells.shape, f32),
            jax.ShapeDtypeStruct((1, 128), f32),
        ),
        name="cell_velocity",
    )(near_slots, own_slots, drag, cells, flat_pos, flat_force)


def wall_kernel(
    cell_slot_ref, patch_slot_ref, target_ref, pos_ref, force_ref, wall_ref, out_ref,
    side_ref, direct_ref, coef_ref, acc_ref, *, near, listed
):
    patch = pl.program_id(0)
    target = target_ref[0]
    points = target.shape[1]
    per_cell = pos_ref.shape[2] // CHUNK
    features = target_features(target)
    for n in range(near):
        slot = cell_slot_ref[patch, n]
        stokes_prepare(pos_ref[slot], force_ref[slot], side_ref, direct_ref, coef_ref, n * per_cell)
    stokes_chunks(features, side_ref, direct_ref, coef_ref, acc_ref, near * per_cell, points)
    flow = stokes_finish(target, acc_ref)
    total = jnp.zeros((32, points), f32)
    for n in range(listed):
        source = wall_ref[patch_slot_ref[patch, n]]
        y = rows8(source[0:3])
        normal = rows8(source[3:6])
        value = rows8(source[6:9])
        weight = -layer_scale * jnp.broadcast_to(source[9:10], y[0].shape)
        value = [weight * v for v in value]
        row = lax.broadcasted_iota(jnp.int32, y[0].shape, 0)
        zero = jnp.zeros_like(y[0])

        def linear(v):
            return source_side(pick(row, [*v, zero, -(y[0] * v[0] + y[1] * v[1] + y[2] * v[2])]))

        s = jnp.dot(distance_features(y, row), features, preferred_element_type=f32)
        along_q = jnp.dot(linear(value), features, preferred_element_type=f32)
        along_n = jnp.dot(linear(normal), features, preferred_element_type=f32)
        root = lax.rsqrt(s)
        square = root * root
        scalar = (along_q * along_n * (square * square * root)).astype(bf16)
        high, middle, low = pieces(pick(row, [*y, jnp.ones_like(y[0])]))
        coef = jnp.concatenate([high, middle, low, zero], axis=0).astype(bf16)
        total = total + jnp.dot(coef, scalar, preferred_element_type=f32)
    moment = total[0:8] + (total[8:16] + total[16:24])
    for i in range(3):
        layer = target[i : i + 1] * moment[3:4] - moment[i : i + 1]
        out_ref[0, i : i + 1, :] = 2.0 * layer + 2.0 * flow[i]


def wall_density(wall_pos, cell_slots, patch_slots, flat_pos, flat_force, ext_wall):
    count, _, points = wall_pos.shape
    near, listed = cell_slots.shape[1], patch_slots.shape[1]
    chunks = near * flat_pos.shape[2] // CHUNK
    whole = pl.BlockSpec(flat_pos.shape, lambda i, *_: (0, 0, 0), pipeline_mode=pl.Buffered(1))
    walls = pl.BlockSpec(ext_wall.shape, lambda i, *_: (0, 0, 0), pipeline_mode=pl.Buffered(1))
    one = pl.BlockSpec((1, 3, points), lambda i, *_: (i, 0, 0))
    return pl.pallas_call(
        functools.partial(wall_kernel, near=near, listed=listed),
        grid_spec=pltpu.PrefetchScalarGridSpec(
            num_scalar_prefetch=2,
            grid=(count,),
            in_specs=[one, whole, whole, walls],
            out_specs=one,
            scratch_shapes=[
                pltpu.VMEM((chunks, CHUNK, 48), bf16),
                pltpu.VMEM((chunks, 16, CHUNK), bf16),
                pltpu.VMEM((chunks, 48, CHUNK), bf16),
                pltpu.VMEM((64, points), f32),
            ],
        ),
        out_shape=jax.ShapeDtypeStruct(wall_pos.shape, f32),
        name="wall_density",
    )(cell_slots, patch_slots, wall_pos, flat_pos, flat_force, ext_wall)


def top_kernel(size_x, size_y, mine_ref, out_ref, row_ref, from_y, from_x, send_y, recv_y, send_x, recv_x):
    me_x, me_y = lax.axis_index("cx"), lax.axis_index("cy")
    barrier = pltpu.get_barrier_semaphore()
    for d in range(1, size_y):
        pl.semaphore_signal(
            barrier, inc=1, device_id=(me_x, lax.rem(me_y + d, size_y)), device_id_type=MESH
        )
    for d in range(1, size_x):
        pl.semaphore_signal(
            barrier, inc=1, device_id=(lax.rem(me_x + d, size_x), me_y), device_id_type=MESH
        )
    pl.semaphore_wait(barrier, size_x + size_y - 2)
    copies = []
    for d in range(1, size_y):
        copy = pltpu.make_async_remote_copy(
            src_ref=mine_ref,
            dst_ref=from_y.at[d - 1],
            send_sem=send_y.at[d - 1],
            recv_sem=recv_y.at[d - 1],
            device_id=(me_x, lax.rem(me_y + d, size_y)),
            device_id_type=MESH,
        )
        copy.start()
        copies.append(copy)
    best = mine_ref[...]
    for d, copy in enumerate(copies):
        copy.wait()
        best = jnp.maximum(best, from_y[d])
    row_ref[...] = best
    copies = []
    for d in range(1, size_x):
        copy = pltpu.make_async_remote_copy(
            src_ref=row_ref,
            dst_ref=from_x.at[d - 1],
            send_sem=send_x.at[d - 1],
            recv_sem=recv_x.at[d - 1],
            device_id=(lax.rem(me_x + d, size_x), me_y),
            device_id_type=MESH,
        )
        copy.start()
        copies.append(copy)
    for d, copy in enumerate(copies):
        copy.wait()
        best = jnp.maximum(best, from_x[d])
    out_ref[...] = best


def top_of_all(mine, size_x, size_y):
    dma = pltpu.SemaphoreType.DMA
    return pl.pallas_call(
        functools.partial(top_kernel, size_x, size_y),
        out_shape=jax.ShapeDtypeStruct(mine.shape, f32),
        in_specs=[pl.BlockSpec(memory_space=pltpu.VMEM)],
        out_specs=pl.BlockSpec(memory_space=pltpu.VMEM),
        scratch_shapes=[
            pltpu.VMEM(mine.shape, f32),
            pltpu.VMEM((size_y - 1, *mine.shape), f32),
            pltpu.VMEM((size_x - 1, *mine.shape), f32),
            dma((size_y - 1,)),
            dma((size_y - 1,)),
            dma((size_x - 1,)),
            dma((size_x - 1,)),
        ],
        compiler_params=pltpu.CompilerParams(collective_id=0, has_side_effects=True),
        name="top_of_all",
    )(mine)


def body(
    cell_pos,
    cell_drag,
    cell_near,
    analysis,
    stiffness,
    synthesis,
    wall_pos,
    wall_normal,
    wall_weight,
    density,
    patch_near,
    cell_to_patch,
):
    row_count = cell_pos.shape[0]
    col_count = cell_pos.shape[1]
    points = cell_pos.shape[3]
    ext_cols = col_count + 2 * HALO
    all_rows = row_count * lax.axis_size("cx")
    all_cols = col_count * lax.axis_size("cy")
    first_row = lax.axis_index("cx") * row_count
    first_col = lax.axis_index("cy") * col_count
    slot = functools.partial(
        local_slot,
        first_row=first_row,
        first_col=first_col,
        all_rows=all_rows,
        all_cols=all_cols,
        ext_cols=ext_cols,
    )
    ext_pos = with_halo(cell_pos, (("cx", 0), ("cy", 1)), HALO)
    ext_force = membrane(ext_pos, analysis, stiffness, synthesis)
    flat_pos = ext_pos.reshape(-1, 3, points)
    flat_force = ext_force.reshape(-1, 3, points)
    count = row_count * col_count
    near_slots = slot(cell_near).reshape(count, -1)
    ids = jnp.arange(count, dtype=jnp.int32)
    own_slots = (ids // col_count + HALO) * ext_cols + ids % col_count + HALO
    velocity, top_square = cell_velocity(
        cell_pos.reshape(count, 3, points),
        cell_drag.reshape(count),
        near_slots,
        own_slots,
        flat_pos,
        flat_force,
    )
    top = jnp.sqrt(top_of_all(top_square, lax.axis_size("cx"), lax.axis_size("cy"))[0, 0])
    step = 1.0 / (top + 1e-06)
    moved_cells = cell_pos + step * velocity.reshape(cell_pos.shape)
    patch_count = wall_pos.shape[0]
    packed = jnp.concatenate([wall_pos, wall_normal, density, wall_weight[:, None, :]], axis=1)
    ext_wall = with_halo(packed, ((("cx", "cy"), 0),), patch_count)
    all_patches = patch_count * lax.axis_size(("cx", "cy"))
    block_start = lax.axis_index(("cx", "cy")) * patch_count
    own_patches = jnp.arange(patch_count, dtype=jnp.int32) + patch_count
    other_slots = (patch_near - block_start + patch_count) % all_patches
    chosen = jnp.concatenate([own_patches[:, None], other_slots], axis=1)
    density_next = wall_density(
        wall_pos, slot(cell_to_patch), chosen, flat_pos, flat_force, ext_wall
    )
    return (moved_cells, density_next)


def solution(mesh):
    placed = (
        P("cx", "cy", None, None),
        P("cx", "cy"),
        P("cx", "cy", None),
        P(),
        P(),
        P(),
        P(("cx", "cy"), None, None),
        P(("cx", "cy"), None, None),
        P(("cx", "cy"), None),
        P(("cx", "cy"), None, None),
        P(("cx", "cy"), None),
        P(("cx", "cy"), None),
    )
    return jax.shard_map(
        body,
        mesh=mesh,
        in_specs=placed,
        out_specs=(P("cx", "cy", None, None), P(("cx", "cy"), None, None)),
        check_vma=False,
    )
```

```python
import functools
import math

import jax
import jax.numpy as jnp
from jax import lax
from jax.experimental import pallas as pl
from jax.experimental.pallas import tpu as pltpu
from jax.sharding import PartitionSpec as P

HALO = 3
WIDTH = 512

soften = 0.25
stokes_scale = 1.0 / (8.0 * math.pi)
layer_scale = 3.0 / (4.0 * math.pi)

MESH = pl.DeviceIdType.MESH
f32 = jnp.float32
bf16 = jnp.bfloat16


def with_halo(value, sides, width):
    for axis, dim in sides:
        size, length = (lax.axis_size(axis), value.shape[dim])
        up = [(i, (i + 1) % size) for i in range(size)]
        down = [(j, i) for i, j in up]
        last = lax.slice_in_dim(value, length - width, length, axis=dim)
        initial = lax.slice_in_dim(value, 0, width, axis=dim)
        before = lax.ppermute(last, axis, up)
        after = lax.ppermute(initial, axis, down)
        value = jnp.concatenate([before, value, after], axis=dim)
    return value


def membrane(positions, analysis, stiffness, synthesis):
    points = positions.shape[-1]
    centred = positions - jnp.mean(positions, axis=-1, keepdims=True)
    flat = centred.reshape(-1, points).astype(jnp.bfloat16)
    coeff = jnp.dot(flat, analysis, preferred_element_type=jnp.float32)
    scaled = (coeff * stiffness[None, :]).astype(jnp.bfloat16)
    force = -jnp.dot(scaled, synthesis, preferred_element_type=jnp.float32)
    return force.reshape(positions.shape)


def local_slot(global_id, first_row, first_col, all_rows, all_cols, ext_cols):
    grid_row = global_id // all_cols
    grid_col = global_id % all_cols
    local_row = (grid_row - first_row + HALO) % all_rows
    local_col = (grid_col - first_col + HALO) % all_cols
    return local_row * ext_cols + local_col


def pieces(value):
    high = value.astype(bf16).astype(f32)
    rest = value - high
    middle = rest.astype(bf16).astype(f32)
    return high, middle, rest - middle


def rows8(points):
    return [jnp.broadcast_to(points[i : i + 1, :], (8, points.shape[1])) for i in range(3)]


def pick(row, values):
    out = jnp.zeros_like(values[0])
    for i, value in enumerate(values):
        out = jnp.where(row == i, value, out)
    return out


def target_features(points):
    x0, x1, x2 = rows8(points)
    row = lax.broadcasted_iota(jnp.int32, x0.shape, 0)
    square = x0 * x0 + x1 * x1 + x2 * x2
    high, middle, low = pieces(pick(row, [x0, x1, x2, square, jnp.ones_like(x0)]))
    return jnp.concatenate([high, high, middle, high, low, middle], axis=0).astype(bf16)


def source_side(value):
    high, middle, low = pieces(value)
    stacked = jnp.concatenate([high, middle, high, low, high, middle], axis=0)
    return stacked.T.astype(bf16)


def distance_features(y, row):
    y0, y1, y2 = y
    square = y0 * y0 + y1 * y1 + y2 * y2 + soften
    return source_side(pick(row, [-2.0 * y0, -2.0 * y1, -2.0 * y2, jnp.ones_like(y0), square]))


def stokes_prepare(source, force, side_ref, coef_ref, base):
    y = rows8(source)
    f = rows8(force)
    row = lax.broadcasted_iota(jnp.int32, y[0].shape, 0)
    along = y[0] * f[0] + y[1] * f[1] + y[2] * f[2]
    square = y[0] * y[0] + y[1] * y[1] + y[2] * y[2]
    f8 = pick(row % 4, [f[0], f[1], f[2], along])
    h1, m1, l1 = pieces(f8 * jnp.where(row < 4, 1.0, y[0]))
    h2, m2, l2 = pieces(f8 * jnp.where(row < 4, y[1], y[2]))
    h3, m3, l3 = pieces(f8 * square)
    points = source.shape[1]
    side_ref[base : base + points] = distance_features(y, row)
    coef_ref[:, base : base + points] = jnp.concatenate(
        [h1, h2, h3, m1, m2, m3, l1, l2, l3], axis=0
    ).astype(bf16)


def stokes_sums(features, side_ref, coef_ref, acc_ref, width):
    side = side_ref[...]
    coef = coef_ref[...]
    for t in range(features.shape[1] // width):
        part = slice(t * width, (t + 1) * width)
        root = lax.rsqrt(jnp.dot(side, features[:, part], preferred_element_type=f32))
        cube = (root * root * root).astype(bf16)
        acc_ref[:, part] = jnp.dot(coef, cube, preferred_element_type=f32)


def stokes_finish(target, acc_ref):
    x = [target[i : i + 1, :] for i in range(3)]
    low = acc_ref[0:8, :] + (acc_ref[24:32, :] + acc_ref[48:56, :])
    high = acc_ref[8:16, :] + (acc_ref[32:40, :] + acc_ref[56:64, :])
    far = acc_ref[16:24, :] + (acc_ref[40:48, :] + acc_ref[64:72, :])
    square = x[0] * x[0] + x[1] * x[1] + x[2] * x[2] + 2.0 * soften

    def contract(block, at):
        out = -block[at + 3 : at + 4]
        for j in range(3):
            out = out + x[j] * block[at + j : at + j + 1]
        return out

    line = contract(low, 0)
    turned = [contract(low, 4), contract(high, 0), contract(high, 4)]
    out = []
    for i in range(3):
        cross = x[0] * low[4 + i : 5 + i] + x[1] * high[i : i + 1] + x[2] * high[4 + i : 5 + i]
        direct = square * low[i : i + 1] + far[i : i + 1] - 2.0 * cross
        out.append(stokes_scale * (direct + x[i] * line - turned[i]))
    return out


def cell_kernel(
    slot_ref, own_ref, drag_ref, target_ref, pos_ref, force_ref, out_ref, top_ref,
    side_ref, coef_ref, acc_ref, *, near
):
    cell = pl.program_id(0)
    target = target_ref[0]
    per_cell = pos_ref.shape[2]
    features = target_features(target)
    for n in range(near):
        slot = slot_ref[cell, n]
        stokes_prepare(pos_ref[slot], force_ref[slot], side_ref, coef_ref, n * per_cell)
    stokes_sums(features, side_ref, coef_ref, acc_ref, min(WIDTH, target.shape[1]))
    own = force_ref[own_ref[cell]]
    drag = drag_ref[cell]
    parts = stokes_finish(target, acc_ref)
    square = jnp.zeros_like(parts[0])
    for i in range(3):
        value = drag * own[i : i + 1] + parts[i]
        out_ref[0, i : i + 1, :] = value
        square = square + value * value
    best = jnp.broadcast_to(jnp.max(square, axis=1, keepdims=True), (1, 128))

    @pl.when(cell == 0)
    def _():
        top_ref[...] = best

    @pl.when(cell > 0)
    def _():
        top_ref[...] = jnp.maximum(top_ref[...], best)


def cell_velocity(cells, drag, near_slots, own_slots, flat_pos, flat_force):
    count, _, points = cells.shape
    near = near_slots.shape[1]
    sources = near * points
    whole = pl.BlockSpec(flat_pos.shape, lambda i, *_: (0, 0, 0), pipeline_mode=pl.Buffered(1))
    one = pl.BlockSpec((1, 3, points), lambda i, *_: (i, 0, 0))
    return pl.pallas_call(
        functools.partial(cell_kernel, near=near),
        grid_spec=pltpu.PrefetchScalarGridSpec(
            num_scalar_prefetch=3,
            grid=(count,),
            in_specs=[one, whole, whole],
            out_specs=[one, pl.BlockSpec((1, 128), lambda i, *_: (0, 0))],
            scratch_shapes=[
                pltpu.VMEM((sources, 48), bf16),
                pltpu.VMEM((72, sources), bf16),
                pltpu.VMEM((72, points), f32),
            ],
        ),
        out_shape=(
            jax.ShapeDtypeStruct(cells.shape, f32),
            jax.ShapeDtypeStruct((1, 128), f32),
        ),
        name="cell_velocity",
    )(near_slots, own_slots, drag, cells, flat_pos, flat_force)


def wall_kernel(
    cell_slot_ref, patch_slot_ref, target_ref, pos_ref, force_ref, wall_ref, out_ref,
    side_ref, coef_ref, acc_ref, layer_ref, moment_ref, *, near, listed
):
    patch = pl.program_id(0)
    target = target_ref[0]
    points = target.shape[1]
    per_cell = pos_ref.shape[2]
    features = target_features(target)
    for n in range(near):
        slot = cell_slot_ref[patch, n]
        stokes_prepare(pos_ref[slot], force_ref[slot], side_ref, coef_ref, n * per_cell)
    stokes_sums(features, side_ref, coef_ref, acc_ref, min(WIDTH, points))
    flow = stokes_finish(target, acc_ref)
    for n in range(listed):
        source = wall_ref[patch_slot_ref[patch, n]]
        y = rows8(source[0:3])
        normal = rows8(source[3:6])
        value = rows8(source[6:9])
        weight = -layer_scale * jnp.broadcast_to(source[9:10], y[0].shape)
        value = [weight * v for v in value]
        row = lax.broadcasted_iota(jnp.int32, y[0].shape, 0)
        zero = jnp.zeros_like(y[0])

        def linear(v):
            return source_side(pick(row, [*v, zero, -(y[0] * v[0] + y[1] * v[1] + y[2] * v[2])]))

        part = slice(n * points, (n + 1) * points)
        layer_ref[0, part] = distance_features(y, row)
        layer_ref[1, part] = linear(value)
        layer_ref[2, part] = linear(normal)
        high, middle, low = pieces(pick(row, [*y, jnp.ones_like(y[0])]))
        moment_ref[:, part] = jnp.concatenate([high, middle, low, zero], axis=0).astype(bf16)
    root = lax.rsqrt(jnp.dot(layer_ref[0], features, preferred_element_type=f32))
    along_q = jnp.dot(layer_ref[1], features, preferred_element_type=f32)
    along_n = jnp.dot(layer_ref[2], features, preferred_element_type=f32)
    square = root * root
    scalar = (along_q * along_n * (square * square * root)).astype(bf16)
    total = jnp.dot(moment_ref[...], scalar, preferred_element_type=f32)
    moment = total[0:8] + (total[8:16] + total[16:24])
    for i in range(3):
        layer = target[i : i + 1] * moment[3:4] - moment[i : i + 1]
        out_ref[0, i : i + 1, :] = 2.0 * layer + 2.0 * flow[i]


def wall_density(wall_pos, cell_slots, patch_slots, flat_pos, flat_force, ext_wall):
    count, _, points = wall_pos.shape
    near, listed = cell_slots.shape[1], patch_slots.shape[1]
    sources = near * flat_pos.shape[2]
    whole = pl.BlockSpec(flat_pos.shape, lambda i, *_: (0, 0, 0), pipeline_mode=pl.Buffered(1))
    walls = pl.BlockSpec(ext_wall.shape, lambda i, *_: (0, 0, 0), pipeline_mode=pl.Buffered(1))
    one = pl.BlockSpec((1, 3, points), lambda i, *_: (i, 0, 0))
    return pl.pallas_call(
        functools.partial(wall_kernel, near=near, listed=listed),
        grid_spec=pltpu.PrefetchScalarGridSpec(
            num_scalar_prefetch=2,
            grid=(count,),
            in_specs=[one, whole, whole, walls],
            out_specs=one,
            scratch_shapes=[
                pltpu.VMEM((sources, 48), bf16),
                pltpu.VMEM((72, sources), bf16),
                pltpu.VMEM((72, points), f32),
                pltpu.VMEM((3, listed * points, 48), bf16),
                pltpu.VMEM((32, listed * points), bf16),
            ],
        ),
        out_shape=jax.ShapeDtypeStruct(wall_pos.shape, f32),
        name="wall_density",
    )(cell_slots, patch_slots, wall_pos, flat_pos, flat_force, ext_wall)


def top_kernel(size_x, size_y, mine_ref, out_ref, row_ref, from_y, from_x, send_y, recv_y, send_x, recv_x):
    me_x, me_y = lax.axis_index("cx"), lax.axis_index("cy")
    barrier = pltpu.get_barrier_semaphore()
    for d in range(1, size_y):
        pl.semaphore_signal(
            barrier, inc=1, device_id=(me_x, lax.rem(me_y + d, size_y)), device_id_type=MESH
        )
    for d in range(1, size_x):
        pl.semaphore_signal(
            barrier, inc=1, device_id=(lax.rem(me_x + d, size_x), me_y), device_id_type=MESH
        )
    pl.semaphore_wait(barrier, size_x + size_y - 2)
    copies = []
    for d in range(1, size_y):
        copy = pltpu.make_async_remote_copy(
            src_ref=mine_ref,
            dst_ref=from_y.at[d - 1],
            send_sem=send_y.at[d - 1],
            recv_sem=recv_y.at[d - 1],
            device_id=(me_x, lax.rem(me_y + d, size_y)),
            device_id_type=MESH,
        )
        copy.start()
        copies.append(copy)
    best = mine_ref[...]
    for d, copy in enumerate(copies):
        copy.wait()
        best = jnp.maximum(best, from_y[d])
    row_ref[...] = best
    copies = []
    for d in range(1, size_x):
        copy = pltpu.make_async_remote_copy(
            src_ref=row_ref,
            dst_ref=from_x.at[d - 1],
            send_sem=send_x.at[d - 1],
            recv_sem=recv_x.at[d - 1],
            device_id=(lax.rem(me_x + d, size_x), me_y),
            device_id_type=MESH,
        )
        copy.start()
        copies.append(copy)
    for d, copy in enumerate(copies):
        copy.wait()
        best = jnp.maximum(best, from_x[d])
    out_ref[...] = best


def top_of_all(mine, size_x, size_y):
    dma = pltpu.SemaphoreType.DMA
    return pl.pallas_call(
        functools.partial(top_kernel, size_x, size_y),
        out_shape=jax.ShapeDtypeStruct(mine.shape, f32),
        in_specs=[pl.BlockSpec(memory_space=pltpu.VMEM)],
        out_specs=pl.BlockSpec(memory_space=pltpu.VMEM),
        scratch_shapes=[
            pltpu.VMEM(mine.shape, f32),
            pltpu.VMEM((size_y - 1, *mine.shape), f32),
            pltpu.VMEM((size_x - 1, *mine.shape), f32),
            dma((size_y - 1,)),
            dma((size_y - 1,)),
            dma((size_x - 1,)),
            dma((size_x - 1,)),
        ],
        compiler_params=pltpu.CompilerParams(collective_id=0, has_side_effects=True),
        name="top_of_all",
    )(mine)


def body(
    cell_pos,
    cell_drag,
    cell_near,
    analysis,
    stiffness,
    synthesis,
    wall_pos,
    wall_normal,
    wall_weight,
    density,
    patch_near,
    cell_to_patch,
):
    row_count = cell_pos.shape[0]
    col_count = cell_pos.shape[1]
    points = cell_pos.shape[3]
    ext_cols = col_count + 2 * HALO
    all_rows = row_count * lax.axis_size("cx")
    all_cols = col_count * lax.axis_size("cy")
    first_row = lax.axis_index("cx") * row_count
    first_col = lax.axis_index("cy") * col_count
    slot = functools.partial(
        local_slot,
        first_row=first_row,
        first_col=first_col,
        all_rows=all_rows,
        all_cols=all_cols,
        ext_cols=ext_cols,
    )
    ext_pos = with_halo(cell_pos, (("cx", 0), ("cy", 1)), HALO)
    ext_force = membrane(ext_pos, analysis, stiffness, synthesis)
    flat_pos = ext_pos.reshape(-1, 3, points)
    flat_force = ext_force.reshape(-1, 3, points)
    count = row_count * col_count
    near_slots = slot(cell_near).reshape(count, -1)
    ids = jnp.arange(count, dtype=jnp.int32)
    own_slots = (ids // col_count + HALO) * ext_cols + ids % col_count + HALO
    velocity, top_square = cell_velocity(
        cell_pos.reshape(count, 3, points),
        cell_drag.reshape(count),
        near_slots,
        own_slots,
        flat_pos,
        flat_force,
    )
    top = jnp.sqrt(top_of_all(top_square, lax.axis_size("cx"), lax.axis_size("cy"))[0, 0])
    step = 1.0 / (top + 1e-06)
    moved_cells = cell_pos + step * velocity.reshape(cell_pos.shape)
    patch_count = wall_pos.shape[0]
    packed = jnp.concatenate([wall_pos, wall_normal, density, wall_weight[:, None, :]], axis=1)
    ext_wall = with_halo(packed, ((("cx", "cy"), 0),), patch_count)
    all_patches = patch_count * lax.axis_size(("cx", "cy"))
    block_start = lax.axis_index(("cx", "cy")) * patch_count
    own_patches = jnp.arange(patch_count, dtype=jnp.int32) + patch_count
    other_slots = (patch_near - block_start + patch_count) % all_patches
    chosen = jnp.concatenate([own_patches[:, None], other_slots], axis=1)
    density_next = wall_density(
        wall_pos, slot(cell_to_patch), chosen, flat_pos, flat_force, ext_wall
    )
    return (moved_cells, density_next)


def solution(mesh):
    placed = (
        P("cx", "cy", None, None),
        P("cx", "cy"),
        P("cx", "cy", None),
        P(),
        P(),
        P(),
        P(("cx", "cy"), None, None),
        P(("cx", "cy"), None, None),
        P(("cx", "cy"), None),
        P(("cx", "cy"), None, None),
        P(("cx", "cy"), None),
        P(("cx", "cy"), None),
    )
    return jax.shard_map(
        body,
        mesh=mesh,
        in_specs=placed,
        out_specs=(P("cx", "cy", None, None), P(("cx", "cy"), None, None)),
        check_vma=False,
    )
```

```python
import functools
import math

import jax
import jax.numpy as jnp
from jax import lax
from jax.experimental import pallas as pl
from jax.experimental.pallas import tpu as pltpu
from jax.sharding import PartitionSpec as P

HALO = 3
WIDTH = 512

soften = 0.25
stokes_scale = 1.0 / (8.0 * math.pi)
layer_scale = 3.0 / (4.0 * math.pi)

MESH = pl.DeviceIdType.MESH
f32 = jnp.float32
bf16 = jnp.bfloat16


def halo_kernel(size_x, size_y, cell_ref, wall_ref, ext_ref, walls_ref, send, recv, local):
    me_x, me_y = lax.axis_index("cx"), lax.axis_index("cy")
    rows, cols = cell_ref.shape[0], cell_ref.shape[1]
    patches = wall_ref.shape[0]

    def side(step, length):
        if step == 1:
            return slice(length - HALO, length), slice(0, HALO)
        if step == 0:
            return slice(0, length), slice(HALO, HALO + length)
        return slice(0, HALO), slice(HALO + length, 2 * HALO + length)

    pieces_out = []
    for dx in (0, 1, -1):
        for dy in (1, -1, 0):
            if dx == 0 and dy == 0:
                continue
            device = (lax.rem(me_x + dx + size_x, size_x), lax.rem(me_y + dy + size_y, size_y))
            (take_x, put_x), (take_y, put_y) = side(dx, rows), side(dy, cols)
            pieces_out.append((cell_ref.at[take_x, take_y], ext_ref.at[put_x, put_y], device))
    flat = me_x * size_y + me_y
    for step, first in ((1, 0), (-1, 2 * patches)):
        other = lax.rem(flat + step + size_x * size_y, size_x * size_y)
        device = (other // size_y, lax.rem(other, size_y))
        pieces_out.append((wall_ref, walls_ref.at[first : first + patches], device))

    barrier = pltpu.get_barrier_semaphore()
    for _, _, device in pieces_out:
        pl.semaphore_signal(barrier, inc=1, device_id=device, device_id_type=MESH)
    pl.semaphore_wait(barrier, len(pieces_out))
    copies = []
    for k, (src, dst, device) in enumerate(pieces_out):
        copy = pltpu.make_async_remote_copy(
            src_ref=src,
            dst_ref=dst,
            send_sem=send.at[k],
            recv_sem=recv.at[k],
            device_id=device,
            device_id_type=MESH,
        )
        copy.start()
        copies.append(copy)
    own = ext_ref.at[HALO : HALO + rows, HALO : HALO + cols]
    copies.append(pltpu.make_async_copy(cell_ref, own, local.at[0]))
    copies[-1].start()
    copies.append(pltpu.make_async_copy(wall_ref, walls_ref.at[patches : 2 * patches], local.at[1]))
    copies[-1].start()
    for copy in copies:
        copy.wait()


def halos(cells, walls, size_x, size_y):
    rows, cols, _, points = cells.shape
    dma = pltpu.SemaphoreType.DMA
    return pl.pallas_call(
        functools.partial(halo_kernel, size_x, size_y),
        out_shape=(
            jax.ShapeDtypeStruct((rows + 2 * HALO, cols + 2 * HALO, 3, points), f32),
            jax.ShapeDtypeStruct((3 * walls.shape[0], *walls.shape[1:]), f32),
        ),
        in_specs=[pl.BlockSpec(memory_space=pltpu.VMEM)] * 2,
        out_specs=[pl.BlockSpec(memory_space=pl.ANY)] * 2,
        scratch_shapes=[dma((10,)), dma((10,)), dma((2,))],
        compiler_params=pltpu.CompilerParams(collective_id=1, has_side_effects=True),
        name="halos",
    )(cells, walls)


def membrane_kernel(pos_ref, analysis_ref, stiffness_ref, synthesis_ref, out_ref, flat_ref):
    count = pos_ref.shape[0]
    for c in range(count):
        flat_ref[3 * c : 3 * c + 3, :] = pos_ref[c]
    value = flat_ref[0 : 3 * count, :]
    centred = (value - jnp.mean(value, axis=1, keepdims=True)).astype(bf16)
    coeff = jnp.dot(centred, analysis_ref[...], preferred_element_type=f32)
    scaled = (coeff * stiffness_ref[...]).astype(bf16)
    flat_ref[0 : 3 * count, :] = -jnp.dot(scaled, synthesis_ref[...], preferred_element_type=f32)
    for c in range(count):
        out_ref[c] = flat_ref[3 * c : 3 * c + 3, :]


def membrane(positions, analysis, stiffness, synthesis):
    count, _, points = positions.shape
    return pl.pallas_call(
        membrane_kernel,
        out_shape=jax.ShapeDtypeStruct(positions.shape, f32),
        in_specs=[pl.BlockSpec(memory_space=pltpu.VMEM)] * 4,
        out_specs=pl.BlockSpec(memory_space=pltpu.VMEM),
        scratch_shapes=[pltpu.VMEM((-(-3 * count // 8) * 8, points), f32)],
        name="membrane",
    )(positions, analysis, stiffness[None, :], synthesis)


def local_slot(global_id, first_row, first_col, all_rows, all_cols, ext_cols):
    grid_row = global_id // all_cols
    grid_col = global_id % all_cols
    local_row = (grid_row - first_row + HALO) % all_rows
    local_col = (grid_col - first_col + HALO) % all_cols
    return local_row * ext_cols + local_col


def pieces(value):
    high = value.astype(bf16).astype(f32)
    rest = value - high
    middle = rest.astype(bf16).astype(f32)
    return high, middle, rest - middle


def rows8(points):
    return [jnp.broadcast_to(points[i : i + 1, :], (8, points.shape[1])) for i in range(3)]


def pick(row, values):
    out = jnp.zeros_like(values[0])
    for i, value in enumerate(values):
        out = jnp.where(row == i, value, out)
    return out


def target_features(points):
    x0, x1, x2 = rows8(points)
    row = lax.broadcasted_iota(jnp.int32, x0.shape, 0)
    square = x0 * x0 + x1 * x1 + x2 * x2
    high, middle, low = pieces(pick(row, [x0, x1, x2, square, jnp.ones_like(x0)]))
    return jnp.concatenate([high, high, middle, high, low, middle], axis=0).astype(bf16)


def source_side(value):
    high, middle, low = pieces(value)
    stacked = jnp.concatenate([high, middle, high, low, high, middle], axis=0)
    return stacked.T.astype(bf16)


def distance_features(y, row):
    y0, y1, y2 = y
    square = y0 * y0 + y1 * y1 + y2 * y2 + soften
    return source_side(pick(row, [-2.0 * y0, -2.0 * y1, -2.0 * y2, jnp.ones_like(y0), square]))


def stokes_prepare(source, force, side_ref, coef_ref, base):
    y = rows8(source)
    f = rows8(force)
    row = lax.broadcasted_iota(jnp.int32, y[0].shape, 0)
    along = y[0] * f[0] + y[1] * f[1] + y[2] * f[2]
    square = y[0] * y[0] + y[1] * y[1] + y[2] * y[2]
    f8 = pick(row % 4, [f[0], f[1], f[2], along])
    h1, m1, l1 = pieces(f8 * jnp.where(row < 4, 1.0, y[0]))
    h2, m2, l2 = pieces(f8 * jnp.where(row < 4, y[1], y[2]))
    h3, m3, l3 = pieces(f8 * square)
    points = source.shape[1]
    side_ref[base : base + points] = distance_features(y, row)
    coef_ref[:, base : base + points] = jnp.concatenate(
        [h1, h2, h3, m1, m2, m3, l1, l2, l3], axis=0
    ).astype(bf16)


def stokes_sums(features, side_ref, coef_ref, acc_ref, width):
    side = side_ref[...]
    coef = coef_ref[...]
    for t in range(features.shape[1] // width):
        part = slice(t * width, (t + 1) * width)
        root = lax.rsqrt(jnp.dot(side, features[:, part], preferred_element_type=f32))
        cube = (root * root * root).astype(bf16)
        acc_ref[:, part] = jnp.dot(coef, cube, preferred_element_type=f32)


def stokes_finish(target, acc_ref):
    x = [target[i : i + 1, :] for i in range(3)]
    low = acc_ref[0:8, :] + (acc_ref[24:32, :] + acc_ref[48:56, :])
    high = acc_ref[8:16, :] + (acc_ref[32:40, :] + acc_ref[56:64, :])
    far = acc_ref[16:24, :] + (acc_ref[40:48, :] + acc_ref[64:72, :])
    square = x[0] * x[0] + x[1] * x[1] + x[2] * x[2] + 2.0 * soften

    def contract(block, at):
        out = -block[at + 3 : at + 4]
        for j in range(3):
            out = out + x[j] * block[at + j : at + j + 1]
        return out

    line = contract(low, 0)
    turned = [contract(low, 4), contract(high, 0), contract(high, 4)]
    out = []
    for i in range(3):
        cross = x[0] * low[4 + i : 5 + i] + x[1] * high[i : i + 1] + x[2] * high[4 + i : 5 + i]
        direct = square * low[i : i + 1] + far[i : i + 1] - 2.0 * cross
        out.append(stokes_scale * (direct + x[i] * line - turned[i]))
    return out


def cell_kernel(
    slot_ref, own_ref, drag_ref, target_ref, pos_ref, force_ref, out_ref, top_ref,
    side_ref, coef_ref, acc_ref, *, near
):
    cell = pl.program_id(0)
    target = target_ref[0]
    per_cell = pos_ref.shape[2]
    features = target_features(target)
    for n in range(near):
        slot = slot_ref[cell, n]
        stokes_prepare(pos_ref[slot], force_ref[slot], side_ref, coef_ref, n * per_cell)
    stokes_sums(features, side_ref, coef_ref, acc_ref, min(WIDTH, target.shape[1]))
    own = force_ref[own_ref[cell]]
    drag = drag_ref[cell]
    parts = stokes_finish(target, acc_ref)
    square = jnp.zeros_like(parts[0])
    for i in range(3):
        value = drag * own[i : i + 1] + parts[i]
        out_ref[0, i : i + 1, :] = value
        square = square + value * value
    best = jnp.broadcast_to(jnp.max(square, axis=1, keepdims=True), (1, 128))

    @pl.when(cell == 0)
    def _():
        top_ref[...] = best

    @pl.when(cell > 0)
    def _():
        top_ref[...] = jnp.maximum(top_ref[...], best)


def cell_velocity(cells, drag, near_slots, own_slots, flat_pos, flat_force):
    count, _, points = cells.shape
    near = near_slots.shape[1]
    sources = near * points
    whole = pl.BlockSpec(flat_pos.shape, lambda i, *_: (0, 0, 0), pipeline_mode=pl.Buffered(1))
    one = pl.BlockSpec((1, 3, points), lambda i, *_: (i, 0, 0))
    return pl.pallas_call(
        functools.partial(cell_kernel, near=near),
        grid_spec=pltpu.PrefetchScalarGridSpec(
            num_scalar_prefetch=3,
            grid=(count,),
            in_specs=[one, whole, whole],
            out_specs=[one, pl.BlockSpec((1, 128), lambda i, *_: (0, 0))],
            scratch_shapes=[
                pltpu.VMEM((sources, 48), bf16),
                pltpu.VMEM((72, sources), bf16),
                pltpu.VMEM((72, points), f32),
            ],
        ),
        out_shape=(
            jax.ShapeDtypeStruct(cells.shape, f32),
            jax.ShapeDtypeStruct((1, 128), f32),
        ),
        name="cell_velocity",
    )(near_slots, own_slots, drag, cells, flat_pos, flat_force)


def wall_kernel(
    cell_slot_ref, patch_slot_ref, target_ref, pos_ref, force_ref, wall_ref, out_ref,
    side_ref, coef_ref, acc_ref, layer_ref, moment_ref, *, near, listed
):
    patch = pl.program_id(0)
    target = target_ref[0]
    points = target.shape[1]
    per_cell = pos_ref.shape[2]
    features = target_features(target)
    for n in range(near):
        slot = cell_slot_ref[patch, n]
        stokes_prepare(pos_ref[slot], force_ref[slot], side_ref, coef_ref, n * per_cell)
    stokes_sums(features, side_ref, coef_ref, acc_ref, min(WIDTH, points))
    flow = stokes_finish(target, acc_ref)
    for n in range(listed):
        source = wall_ref[patch_slot_ref[patch, n]]
        y = rows8(source[0:3])
        normal = rows8(source[3:6])
        value = rows8(source[6:9])
        weight = -layer_scale * jnp.broadcast_to(source[9:10], y[0].shape)
        value = [weight * v for v in value]
        row = lax.broadcasted_iota(jnp.int32, y[0].shape, 0)
        zero = jnp.zeros_like(y[0])

        def linear(v):
            return source_side(pick(row, [*v, zero, -(y[0] * v[0] + y[1] * v[1] + y[2] * v[2])]))

        part = slice(n * points, (n + 1) * points)
        layer_ref[0, part] = distance_features(y, row)
        layer_ref[1, part] = linear(value)
        layer_ref[2, part] = linear(normal)
        high, middle, low = pieces(pick(row, [*y, jnp.ones_like(y[0])]))
        moment_ref[:, part] = jnp.concatenate([high, middle, low, zero], axis=0).astype(bf16)
    root = lax.rsqrt(jnp.dot(layer_ref[0], features, preferred_element_type=f32))
    along_q = jnp.dot(layer_ref[1], features, preferred_element_type=f32)
    along_n = jnp.dot(layer_ref[2], features, preferred_element_type=f32)
    square = root * root
    scalar = (along_q * along_n * (square * square * root)).astype(bf16)
    total = jnp.dot(moment_ref[...], scalar, preferred_element_type=f32)
    moment = total[0:8] + (total[8:16] + total[16:24])
    for i in range(3):
        layer = target[i : i + 1] * moment[3:4] - moment[i : i + 1]
        out_ref[0, i : i + 1, :] = 2.0 * layer + 2.0 * flow[i]


def wall_density(wall_pos, cell_slots, patch_slots, flat_pos, flat_force, ext_wall):
    count, _, points = wall_pos.shape
    near, listed = cell_slots.shape[1], patch_slots.shape[1]
    sources = near * flat_pos.shape[2]
    whole = pl.BlockSpec(flat_pos.shape, lambda i, *_: (0, 0, 0), pipeline_mode=pl.Buffered(1))
    walls = pl.BlockSpec(ext_wall.shape, lambda i, *_: (0, 0, 0), pipeline_mode=pl.Buffered(1))
    one = pl.BlockSpec((1, 3, points), lambda i, *_: (i, 0, 0))
    return pl.pallas_call(
        functools.partial(wall_kernel, near=near, listed=listed),
        grid_spec=pltpu.PrefetchScalarGridSpec(
            num_scalar_prefetch=2,
            grid=(count,),
            in_specs=[one, whole, whole, walls],
            out_specs=one,
            scratch_shapes=[
                pltpu.VMEM((sources, 48), bf16),
                pltpu.VMEM((72, sources), bf16),
                pltpu.VMEM((72, points), f32),
                pltpu.VMEM((3, listed * points, 48), bf16),
                pltpu.VMEM((32, listed * points), bf16),
            ],
        ),
        out_shape=jax.ShapeDtypeStruct(wall_pos.shape, f32),
        name="wall_density",
    )(cell_slots, patch_slots, wall_pos, flat_pos, flat_force, ext_wall)


def top_kernel(size_x, size_y, mine_ref, out_ref, row_ref, from_y, from_x, send_y, recv_y, send_x, recv_x):
    me_x, me_y = lax.axis_index("cx"), lax.axis_index("cy")
    barrier = pltpu.get_barrier_semaphore()
    for d in range(1, size_y):
        pl.semaphore_signal(
            barrier, inc=1, device_id=(me_x, lax.rem(me_y + d, size_y)), device_id_type=MESH
        )
    for d in range(1, size_x):
        pl.semaphore_signal(
            barrier, inc=1, device_id=(lax.rem(me_x + d, size_x), me_y), device_id_type=MESH
        )
    pl.semaphore_wait(barrier, size_x + size_y - 2)
    copies = []
    for d in range(1, size_y):
        copy = pltpu.make_async_remote_copy(
            src_ref=mine_ref,
            dst_ref=from_y.at[d - 1],
            send_sem=send_y.at[d - 1],
            recv_sem=recv_y.at[d - 1],
            device_id=(me_x, lax.rem(me_y + d, size_y)),
            device_id_type=MESH,
        )
        copy.start()
        copies.append(copy)
    best = mine_ref[...]
    for d, copy in enumerate(copies):
        copy.wait()
        best = jnp.maximum(best, from_y[d])
    row_ref[...] = best
    copies = []
    for d in range(1, size_x):
        copy = pltpu.make_async_remote_copy(
            src_ref=row_ref,
            dst_ref=from_x.at[d - 1],
            send_sem=send_x.at[d - 1],
            recv_sem=recv_x.at[d - 1],
            device_id=(lax.rem(me_x + d, size_x), me_y),
            device_id_type=MESH,
        )
        copy.start()
        copies.append(copy)
    for d, copy in enumerate(copies):
        copy.wait()
        best = jnp.maximum(best, from_x[d])
    out_ref[...] = best


def top_of_all(mine, size_x, size_y):
    dma = pltpu.SemaphoreType.DMA
    return pl.pallas_call(
        functools.partial(top_kernel, size_x, size_y),
        out_shape=jax.ShapeDtypeStruct(mine.shape, f32),
        in_specs=[pl.BlockSpec(memory_space=pltpu.VMEM)],
        out_specs=pl.BlockSpec(memory_space=pltpu.VMEM),
        scratch_shapes=[
            pltpu.VMEM(mine.shape, f32),
            pltpu.VMEM((size_y - 1, *mine.shape), f32),
            pltpu.VMEM((size_x - 1, *mine.shape), f32),
            dma((size_y - 1,)),
            dma((size_y - 1,)),
            dma((size_x - 1,)),
            dma((size_x - 1,)),
        ],
        compiler_params=pltpu.CompilerParams(collective_id=0, has_side_effects=True),
        name="top_of_all",
    )(mine)


def body(
    cell_pos,
    cell_drag,
    cell_near,
    analysis,
    stiffness,
    synthesis,
    wall_pos,
    wall_normal,
    wall_weight,
    density,
    patch_near,
    cell_to_patch,
):
    row_count = cell_pos.shape[0]
    col_count = cell_pos.shape[1]
    points = cell_pos.shape[3]
    ext_cols = col_count + 2 * HALO
    all_rows = row_count * lax.axis_size("cx")
    all_cols = col_count * lax.axis_size("cy")
    first_row = lax.axis_index("cx") * row_count
    first_col = lax.axis_index("cy") * col_count
    slot = functools.partial(
        local_slot,
        first_row=first_row,
        first_col=first_col,
        all_rows=all_rows,
        all_cols=all_cols,
        ext_cols=ext_cols,
    )
    packed = jnp.concatenate([wall_pos, wall_normal, density, wall_weight[:, None, :]], axis=1)
    ext_pos, ext_wall = halos(cell_pos, packed, lax.axis_size("cx"), lax.axis_size("cy"))
    flat_pos = ext_pos.reshape(-1, 3, points)
    flat_force = membrane(flat_pos, analysis, stiffness, synthesis)
    count = row_count * col_count
    near_slots = slot(cell_near).reshape(count, -1)
    ids = jnp.arange(count, dtype=jnp.int32)
    own_slots = (ids // col_count + HALO) * ext_cols + ids % col_count + HALO
    velocity, top_square = cell_velocity(
        cell_pos.reshape(count, 3, points),
        cell_drag.reshape(count),
        near_slots,
        own_slots,
        flat_pos,
        flat_force,
    )
    top = jnp.sqrt(top_of_all(top_square, lax.axis_size("cx"), lax.axis_size("cy"))[0, 0])
    step = 1.0 / (top + 1e-06)
    moved_cells = cell_pos + step * velocity.reshape(cell_pos.shape)
    patch_count = wall_pos.shape[0]
    all_patches = patch_count * lax.axis_size(("cx", "cy"))
    block_start = lax.axis_index(("cx", "cy")) * patch_count
    own_patches = jnp.arange(patch_count, dtype=jnp.int32) + patch_count
    other_slots = (patch_near - block_start + patch_count) % all_patches
    chosen = jnp.concatenate([own_patches[:, None], other_slots], axis=1)
    density_next = wall_density(
        wall_pos, slot(cell_to_patch), chosen, flat_pos, flat_force, ext_wall
    )
    return (moved_cells, density_next)


def solution(mesh):
    placed = (
        P("cx", "cy", None, None),
        P("cx", "cy"),
        P("cx", "cy", None),
        P(),
        P(),
        P(),
        P(("cx", "cy"), None, None),
        P(("cx", "cy"), None, None),
        P(("cx", "cy"), None),
        P(("cx", "cy"), None, None),
        P(("cx", "cy"), None),
        P(("cx", "cy"), None),
    )
    return jax.shard_map(
        body,
        mesh=mesh,
        in_specs=placed,
        out_specs=(P("cx", "cy", None, None), P(("cx", "cy"), None, None)),
        check_vma=False,
    )
```
